128 devices in a mesh: block: 8 (over y, core), row: 16 (over x, z).
Axes of the slice: x: 4, y: 4, z: 4, core: 2. Of those that a mesh axis runs over, the one named last changes fastest.
Arguments:
- snapshots: bfloat16 [32768, 2048], P('block', 'row'), may hold values from -6 to 6
- usable_frame_tallies: int32 [128], replicated, may hold values from 64 to 256, as said below
- retained_frequency_slots: int32 [64], replicated, may hold values from 0 to 127, as said below
- modes: bfloat16 [64, 2, 2048, 512], P('block', None, 'row'), may hold values from -0.09375 to 0.09375
Outputs:
- coefficients: float32 [128, 2, 64, 512], P('row', None, 'block')
- energy: float32 [64, 512], P('block')
The draws below stay inside these ranges and needn't reach their ends.
Inputs may be any that keep to these rules, and one draw needn't show every extreme that they name: Only the first usable_frame_tallies[b] snapshots of block b are valid; some block is full. `retained_frequency_slots`: 64 distinct bins in increasing order; bin 0 and bin 256 // 2 - 1 are always kept.
All inputs are finite; a program needn't handle non-finite values.
Results may differ from the reference program's by a relative error of at most 0.004.
Values may be sent and summed in bfloat16 or wider, within the bound.
No kernel may reach another device: no remote copies, remote signals or barrier semaphores. Data moves between devices by JAX's collectives and lax.ppermute only.
A program may use at most 64 MiB of HBM per device.

```python
import jax
import jax.numpy as jnp
from jax import lax

FRAMES_PER_SEG = 256
K = 64
M = 512
BLOCKS = 128
SNAPS = 32768
X = 2048


def draw_usable_frame_tallies(key, part):
    first_key, second_key = jax.random.split(key)
    values = jax.random.randint(first_key, (BLOCKS,), FRAMES_PER_SEG // 4, FRAMES_PER_SEG + 1, dtype=jnp.int32)
    complete_block = jax.random.randint(second_key, (), 0, BLOCKS, dtype=jnp.int32)
    places = jnp.arange(BLOCKS, dtype=jnp.int32)
    return jnp.where(places == complete_block, FRAMES_PER_SEG, values).astype(jnp.int32)


def draw_retained_frequency_slots(key, part):
    shuffled = jax.random.permutation(key, FRAMES_PER_SEG // 2 - 2) + 1
    chosen = shuffled[:K - 2].astype(jnp.int32)
    edges = jnp.array([0, FRAMES_PER_SEG // 2 - 1], dtype=jnp.int32)
    return jnp.sort(jnp.concatenate([edges, chosen])).astype(jnp.int32)


def spiked(values, stream_key, source, target, parts, factor):
    def block_of(axis_at):
        return (jnp.arange(values.shape[axis_at]) // (values.shape[axis_at] // parts)).reshape((-1,) + (1,) * (values.ndim - 1 - axis_at))

    first = jax.random.permutation(stream_key, parts)[block_of(target)]
    second = (block_of(target) + parts // 2) % parts
    return jnp.where((block_of(source) == first) | (block_of(source) == second), factor * values, values)


def shard_levels(key, dims, cuts, least, largest):
    def one(axis_at, parts):
        draws = jax.random.uniform(jax.random.fold_in(jax.random.fold_in(key, 6), axis_at), (parts,), jnp.float32, least / len(cuts), largest / len(cuts))
        return jnp.repeat(jnp.exp(draws), dims[axis_at] // parts).reshape((-1,) + (1,) * (len(dims) - axis_at - 1))

    gain = one(*cuts[0])
    for cut in cuts[1:]:
        gain = gain * one(*cut)
    return gain


def gaussian(own_key, extent, scale, bound, pieces=(), kind=jnp.bfloat16):
    gain = shard_levels(own_key, extent, pieces, -0.22, 0.18) if pieces else 1.0
    entries = jax.random.normal(own_key, extent, jnp.float32) * scale * gain
    return jnp.minimum(jnp.maximum(entries, -bound), bound).astype(kind)


def noise_with(own_key, dims, deviation, reach, cuts, heavy, held_as=jnp.bfloat16):
    values = deviation * jax.random.normal(own_key, dims, jnp.float32)
    if cuts:
        values = values * shard_levels(own_key, dims, cuts, -0.22, 0.18)
    return jnp.clip(spiked(values, jax.random.fold_in(own_key, 3), *heavy), -reach, reach).astype(held_as)


def setup_inputs(seed: int = 0) -> dict:
    keys = jax.random.split(jax.random.key(seed), 5)
    return {
        "snapshots": noise_with(keys[0], (SNAPS, X), 1.0, 6.0, ((0, 8), (1, 16)), (1, 0, 16, 2.0)),
        "usable_frame_tallies": draw_usable_frame_tallies(jax.random.fold_in(keys[4], 71), 0),
        "retained_frequency_slots": draw_retained_frequency_slots(jax.random.fold_in(keys[4], 71), 0),
        "modes": gaussian(keys[3], (K, 2, X, M), (2 * X) ** -0.5, 0.09375, ((0, 8), (2, 16))),
    }


def window_table(usable_frame_tallies, retained_frequency_slots):
    recording_epochs = jnp.arange(FRAMES_PER_SEG, dtype=jnp.int32)
    lengths = usable_frame_tallies.astype(jnp.float32)[:, None]
    frequency_power_statistics = recording_epochs.astype(jnp.float32)[None, :]
    domain_grid_locations = recording_epochs[None, :] < usable_frame_tallies[:, None]
    window = jnp.where(domain_grid_locations, jnp.sin(jnp.pi * (frequency_power_statistics + 0.5) / lengths) ** 2, 0.0)
    scaling = 1.0 / jnp.sqrt(lax.optimization_barrier(jnp.sum(window * window, axis=1, keepdims=True)))
    remaining_matrix_lines = retained_frequency_slots[:, None] * recording_epochs[None, :] % FRAMES_PER_SEG
    phase = remaining_matrix_lines.astype(jnp.float32) * (2.0 * jnp.pi / FRAMES_PER_SEG)
    trig = jnp.stack([jnp.cos(phase), -jnp.sin(phase)])
    return ((scaling * window)[:, None, None, :] * trig[None]).astype(jnp.bfloat16)

def reference(snapshots, usable_frame_tallies, retained_frequency_slots, modes):
    table = window_table(usable_frame_tallies, retained_frequency_slots)
    blocks_data = snapshots.reshape(BLOCKS, FRAMES_PER_SEG, X)

    def transform(pair):
        weights, samples = pair
        inner_product = jnp.dot(weights.reshape(2 * K, FRAMES_PER_SEG), samples, preferred_element_type=jnp.float32)
        return inner_product.astype(jnp.bfloat16).reshape(2, K, X)
    spectra = lax.map(transform, (table, blocks_data))
    by_freq = jnp.moveaxis(spectra, 2, 0)

    def project(pair):
        spectrum, mode_rows = pair
        real_part = spectrum[:, 0]
        imag_part = spectrum[:, 1]
        stacked = jnp.concatenate([jnp.concatenate([real_part, imag_part], axis=-1), jnp.concatenate([imag_part, -real_part], axis=-1)], axis=0)
        result = jnp.dot(stacked, mode_rows.reshape(2 * X, M), preferred_element_type=jnp.float32)
        return result.reshape(2, BLOCKS, M)
    projected = lax.map(project, (by_freq, modes))
    coefficients = jnp.transpose(projected, (2, 1, 0, 3))
    weights = usable_frame_tallies.astype(jnp.float32)
    power = coefficients[:, 0] ** 2 + coefficients[:, 1] ** 2
    energy = lax.optimization_barrier(jnp.sum(weights[:, None, None] * power, axis=0)) / jnp.sum(weights)
    return (coefficients, energy)
```

```python
import jax
import jax.numpy as jnp
from jax import lax
from jax.sharding import PartitionSpec as P

FRAMES_PER_SEG = 256


def window_table(usable_frame_tallies, retained_frequency_slots):
    recording_epochs = jnp.arange(FRAMES_PER_SEG, dtype=jnp.int32)
    lengths = usable_frame_tallies.astype(jnp.float32)[:, None]
    frequency_power_statistics = recording_epochs.astype(jnp.float32)[None, :]
    domain_grid_locations = recording_epochs[None, :] < usable_frame_tallies[:, None]
    window = jnp.where(
        domain_grid_locations,
        jnp.sin(jnp.pi * (frequency_power_statistics + 0.5) / lengths) ** 2,
        0.0,
    )
    scaling = 1.0 / jnp.sqrt(jnp.sum(window * window, axis=1, keepdims=True))
    remaining_matrix_lines = (
        retained_frequency_slots[:, None] * recording_epochs[None, :] % FRAMES_PER_SEG
    )
    phase = remaining_matrix_lines.astype(jnp.float32) * (2.0 * jnp.pi / FRAMES_PER_SEG)
    trig = jnp.stack([jnp.cos(phase), -jnp.sin(phase)])
    return ((scaling * window)[:, None, None, :] * trig[None]).astype(jnp.bfloat16)


def shards(snapshots, usable_frame_tallies, retained_frequency_slots, modes):
    own_blocks = snapshots.shape[0] // FRAMES_PER_SEG
    row_width = snapshots.shape[1]
    first_block = lax.axis_index("block") * own_blocks
    own_counts = lax.dynamic_slice_in_dim(usable_frame_tallies, first_block, own_blocks, 0)
    table = window_table(own_counts, retained_frequency_slots)
    blocks_data = snapshots.reshape(own_blocks, FRAMES_PER_SEG, row_width)
    spectra = jnp.einsum(
        "bckt,btx->bckx", table, blocks_data, preferred_element_type=jnp.float32
    ).astype(jnp.bfloat16)
    moved = lax.all_to_all(spectra, "block", split_axis=2, concat_axis=0, tiled=True)
    real_part = moved[:, 0]
    imag_part = moved[:, 1]
    stacked_left = jnp.stack(
        [
            jnp.concatenate([real_part, imag_part], axis=-1),
            jnp.concatenate([imag_part, -real_part], axis=-1),
        ],
        axis=1,
    )
    mode_rows = modes.reshape(modes.shape[0], 2 * row_width, modes.shape[3])
    blocks_all = stacked_left.shape[0]
    rows = lax.axis_size("row")
    share_rows = blocks_all // rows
    first_row = lax.axis_index("row") * share_rows
    weights = usable_frame_tallies.astype(jnp.float32)
    total_weight = jnp.sum(weights)
    partial = jnp.einsum(
        "bckx,kxm->kcbm", stacked_left, mode_rows, preferred_element_type=jnp.float32
    ).astype(jnp.bfloat16)
    k, c, _, m = partial.shape
    partial = partial.reshape(k, c, rows, share_rows, m).transpose(2, 0, 1, 3, 4)
    pieces = lax.all_to_all(partial, "row", split_axis=0, concat_axis=0, tiled=True)
    total = jnp.sum(pieces.astype(jnp.float32), axis=0)
    coefficients = total.transpose(2, 1, 0, 3)
    own_weights = lax.dynamic_slice_in_dim(weights, first_row, share_rows, 0)
    power = total[:, 0] ** 2 + total[:, 1] ** 2
    energy = jnp.sum(own_weights[None, :, None] * power, axis=1)
    copies = jnp.broadcast_to(energy[None], (rows,) + energy.shape)
    energy = jnp.sum(lax.all_to_all(copies, "row", 0, 0, tiled=True), axis=0) / total_weight
    return (coefficients, energy)


def solution(mesh):
    placed = (P("block", "row"), P(), P(), P("block", None, "row", None))
    return jax.shard_map(
        shards,
        mesh=mesh,
        in_specs=placed,
        out_specs=(P("row", None, "block", None), P("block", None)),
        check_vma=False,
    )
```

```python
import functools

import jax
import jax.numpy as jnp
from jax import lax
from jax.experimental import pallas as pl
from jax.experimental.pallas import tpu as pltpu
from jax.sharding import PartitionSpec as P

FRAMES_PER_SEG = 256
SIDE = 4
VMEM = pl.BlockSpec(memory_space=pltpu.VMEM)
SMEM = pl.BlockSpec(memory_space=pltpu.SMEM)
bf16, f32 = jnp.bfloat16, jnp.float32


def window_table(usable_frame_tallies, retained_frequency_slots):
    recording_epochs = jnp.arange(FRAMES_PER_SEG, dtype=jnp.int32)
    lengths = usable_frame_tallies.astype(jnp.float32)[:, None]
    frequency_power_statistics = recording_epochs.astype(jnp.float32)[None, :]
    domain_grid_locations = recording_epochs[None, :] < usable_frame_tallies[:, None]
    window = jnp.where(
        domain_grid_locations,
        jnp.sin(jnp.pi * (frequency_power_statistics + 0.5) / lengths) ** 2,
        0.0,
    )
    scaling = 1.0 / jnp.sqrt(jnp.sum(window * window, axis=1, keepdims=True))
    remaining_matrix_lines = (
        retained_frequency_slots[:, None] * recording_epochs[None, :] % FRAMES_PER_SEG
    )
    phase = remaining_matrix_lines.astype(jnp.float32) * (2.0 * jnp.pi / FRAMES_PER_SEG)
    trig = jnp.stack([jnp.cos(phase), -jnp.sin(phase)])
    return ((scaling * window)[:, None, None, :] * trig[None]).astype(jnp.bfloat16)


def grid_place():
    row = lax.axis_index("row")
    return row // SIDE, row % SIDE


def project_kernel(spectra, modes, *refs):
    outs, acc = refs[:-1], refs[-1]
    x, z = grid_place()
    freqs, points, width = spectra.shape[1], spectra.shape[4], modes.shape[2]
    blocks = spectra.shape[0] * spectra.shape[3]
    half = freqs // 2
    for k in range(freqs):
        real = spectra[:, k, 0].reshape(blocks, points)
        imag = spectra[:, k, 1].reshape(blocks, points)
        left = jnp.concatenate(
            [
                jnp.concatenate([real, imag], axis=1),
                jnp.concatenate([imag, -real], axis=1),
            ],
            axis=0,
        )
        slot = k % 2
        acc[slot] = jnp.dot(left, modes[k], preferred_element_type=f32).reshape(acc.shape[1:])
        for i in range(SIDE):
            if k < half:
                piece = acc[slot, :, (x + i) % SIDE]
                out = outs[i]
            else:
                piece = acc[slot, :, :, (z + i) % SIDE]
                out = outs[SIDE + i]
            out[k % half] = piece.reshape(2, -1, width).astype(out.dtype)


def project(spectra, modes):
    freqs, width = modes.shape[0], modes.shape[2]
    blocks = spectra.shape[0] * spectra.shape[3]
    piece = (freqs // 2, 2, blocks // SIDE, width)
    shapes = [jax.ShapeDtypeStruct(piece, f32 if i == 0 else bf16) for i in range(SIDE)] * 2
    return pl.pallas_call(
        project_kernel,
        out_shape=shapes,
        in_specs=[VMEM, VMEM],
        out_specs=[VMEM] * len(shapes),
        scratch_shapes=[
            pltpu.VMEM((2, 2, SIDE, SIDE, blocks // (SIDE * SIDE), width), f32)
        ],
        compiler_params=pltpu.CompilerParams(vmem_limit_bytes=32 << 20),
        name="project",
    )(spectra, modes)


def fold_kernel(along_x, own, first, second, third, *refs):
    outs, acc = refs[:-1], refs[-1]
    x, z = grid_place()
    place = x if along_x else z
    width = own.shape[3]
    for k in range(own.shape[0]):
        total = own[k] + first[k].astype(f32) + second[k].astype(f32) + third[k].astype(f32)
        acc[k % 2] = total.reshape(acc.shape[1:])
        for i in range(SIDE):
            piece = acc[k % 2, :, (place + i) % SIDE].reshape(-1, width)
            outs[i][k] = piece.astype(outs[i].dtype)


def fold(along_x, parts):
    freqs, _, blocks, width = parts[0].shape
    shapes = [
        jax.ShapeDtypeStruct((freqs, 2 * blocks // SIDE, width), f32 if i == 0 else bf16)
        for i in range(SIDE)
    ]
    return pl.pallas_call(
        functools.partial(fold_kernel, along_x),
        out_shape=shapes,
        in_specs=[VMEM] * SIDE,
        out_specs=[VMEM] * SIDE,
        scratch_shapes=[pltpu.VMEM((2, 2, SIDE, blocks // SIDE, width), f32)],
        compiler_params=pltpu.CompilerParams(vmem_limit_bytes=32 << 20),
        name="fold_x" if along_x else "fold_z",
    )(*parts)


def finish_kernel(tallies, *refs):
    parts, (coefficients, energy) = refs[: 2 * SIDE], refs[2 * SIDE :]
    blocks, _, freqs, width = coefficients.shape
    first = lax.axis_index("row") * blocks
    places = lax.broadcasted_iota(jnp.int32, (blocks, width), 0)
    weights = jnp.zeros((blocks, width), f32)
    for j in range(blocks):
        weights = jnp.where(places == j, tallies[first + j].astype(f32), weights)
    half = freqs // 2
    for k in range(freqs):
        group = parts[SIDE * (k // half) : SIDE * (k // half) + SIDE]
        total = sum(part[k % half].astype(f32) for part in group)
        real, imag = total[:blocks], total[blocks:]
        coefficients[:, 0, k, :] = real
        coefficients[:, 1, k, :] = imag
        power = jnp.sum(weights * (real * real + imag * imag), axis=0, keepdims=True)
        energy[:, k : k + 1, :] = jnp.broadcast_to(power[None], (energy.shape[0], 1, width))


def finish(tallies, rows, parts):
    half, blocks2, width = parts[0].shape
    return pl.pallas_call(
        finish_kernel,
        out_shape=[
            jax.ShapeDtypeStruct((blocks2 // 2, 2, 2 * half, width), f32),
            jax.ShapeDtypeStruct((rows, 2 * half, width), f32),
        ],
        in_specs=[SMEM] + [VMEM] * len(parts),
        out_specs=[VMEM, VMEM],
        compiler_params=pltpu.CompilerParams(vmem_limit_bytes=32 << 20),
        name="finish",
    )(tallies, *parts)


def mean_kernel(parts, tallies, energy):
    weight = jnp.sum(tallies[...].astype(f32), axis=1, keepdims=True)
    energy[...] = jnp.sum(parts[...], axis=0) / weight


def shards(snapshots, usable_frame_tallies, retained_frequency_slots, modes):
    own_blocks = snapshots.shape[0] // FRAMES_PER_SEG
    row_width = snapshots.shape[1]
    rows = lax.axis_size("row")
    groups = lax.axis_size("block")
    first_block = lax.axis_index("block") * own_blocks
    own_counts = lax.dynamic_slice_in_dim(usable_frame_tallies, first_block, own_blocks, 0)
    table = window_table(own_counts, retained_frequency_slots)
    blocks_data = snapshots.reshape(own_blocks, FRAMES_PER_SEG, row_width)
    spectra = jnp.einsum(
        "bckt,btx->kcbx", table, blocks_data, preferred_element_type=jnp.float32
    ).astype(jnp.bfloat16)
    spectra = spectra.reshape((groups, -1) + spectra.shape[1:])
    moved = lax.all_to_all(spectra, "block", split_axis=0, concat_axis=0, tiled=True)

    def along(value, dx, dz):
        pairs = [
            (x * SIDE + z, (x + dx) % SIDE * SIDE + (z + dz) % SIDE)
            for x in range(SIDE)
            for z in range(SIDE)
        ]
        return lax.ppermute(value, "row", pairs)

    mode_rows = modes.reshape(modes.shape[0], 2 * row_width, modes.shape[3])
    pieces = project(moved, mode_rows)
    by_x = [pieces[0]] + [along(pieces[i], i, 0) for i in range(1, SIDE)]
    by_z = [pieces[SIDE]] + [along(pieces[SIDE + i], 0, i) for i in range(1, SIDE)]
    from_x = fold(False, by_x)
    from_z = fold(True, by_z)
    last = [from_x[0]] + [along(from_x[i], 0, i) for i in range(1, SIDE)]
    last += [from_z[0]] + [along(from_z[i], i, 0) for i in range(1, SIDE)]
    coefficients, energy_parts = finish(usable_frame_tallies, rows, last)
    swapped = lax.all_to_all(energy_parts, "row", 0, 0, tiled=True)
    energy = pl.pallas_call(
        mean_kernel,
        out_shape=jax.ShapeDtypeStruct(energy_parts.shape[1:], f32),
        in_specs=[VMEM, VMEM],
        out_specs=VMEM,
        name="mean",
    )(swapped, usable_frame_tallies.reshape(1, -1))
    return (coefficients, energy)


def solution(mesh):
    placed = (P("block", "row"), P(), P(), P("block", None, "row", None))
    return jax.shard_map(
        shards,
        mesh=mesh,
        in_specs=placed,
        out_specs=(P("row", None, "block", None), P("block", None)),
        check_vma=False,
    )
```

```python
import jax
import jax.numpy as jnp
from jax import lax
from jax.experimental import pallas as pl
from jax.experimental.pallas import tpu as pltpu
from jax.sharding import PartitionSpec as P

FRAMES_PER_SEG = 256
FARTHEST_FIRST = (2, 1, 3)
PARTS = 4
SIDE = 4
VMEM = pl.BlockSpec(memory_space=pltpu.VMEM)
SMEM = pl.BlockSpec(memory_space=pltpu.SMEM)
SMALL = 8 << 20
bf16, f32 = jnp.bfloat16, jnp.float32


def transform_kernel(
    tallies_hbm, slots_hbm, snapshots_hbm, spectra, acc, tallies, slots, snapshots, sems
):
    copies = [
        pltpu.make_async_copy(tallies_hbm, tallies, sems.at[0]),
        pltpu.make_async_copy(slots_hbm, slots, sems.at[1]),
    ]
    share = snapshots.shape[0] // PARTS
    for part in range(PARTS):
        rows = pl.ds(part * share, share)
        copies.append(
            pltpu.make_async_copy(
                snapshots_hbm.at[rows, :], snapshots.at[rows, :], sems.at[2 + part]
            )
        )
    for copy in copies:
        copy.start()
    copies[0].wait()
    copies[1].wait()
    freqs, _, blocks, points = spectra.shape
    start = lax.axis_index("block") * blocks
    spots = lax.broadcasted_iota(jnp.int32, (blocks, FRAMES_PER_SEG), 0)
    lengths = jnp.zeros((blocks, FRAMES_PER_SEG), jnp.int32)
    for j in range(blocks):
        lengths = jnp.where(spots == j, tallies[start + j], lengths)
    times = lax.broadcasted_iota(jnp.int32, (blocks, FRAMES_PER_SEG), 1)
    angle = jnp.pi * (times.astype(f32) + 0.5) / lengths.astype(f32)
    window = jnp.where(times < lengths, jnp.sin(angle) ** 2, 0.0)
    window = window * (1.0 / jnp.sqrt(jnp.sum(window * window, axis=1, keepdims=True)))
    turns = lax.dot_general(
        slots[...].astype(f32).astype(bf16),
        times[:1].astype(f32).astype(bf16),
        (((0,), (0,)), ((), ())),
        preferred_element_type=f32,
    )
    turns = (turns.astype(jnp.int32) % FRAMES_PER_SEG).astype(f32)
    phase = turns * (2.0 * jnp.pi / FRAMES_PER_SEG)
    waves = jnp.concatenate([jnp.cos(phase), -jnp.sin(phase)], axis=0)
    for j in range(blocks):
        if j % (blocks // PARTS) == 0:
            copies[2 + j // (blocks // PARTS)].wait()
        table = (window[j : j + 1] * waves).astype(bf16)
        frames = snapshots[j * FRAMES_PER_SEG : (j + 1) * FRAMES_PER_SEG, :]
        acc[pl.ds(j, 2 * freqs, stride=blocks), :] = jnp.dot(
            table, frames, preferred_element_type=f32
        )
    for c in range(2):
        rows = acc[c * freqs * blocks : (c + 1) * freqs * blocks, :]
        spectra[:, c] = rows.reshape(freqs, blocks, points).astype(bf16)


def transform(tallies, slots, snapshots):
    blocks, points = snapshots.shape[0] // FRAMES_PER_SEG, snapshots.shape[1]
    freqs = slots.shape[0]
    return pl.pallas_call(
        transform_kernel,
        out_shape=jax.ShapeDtypeStruct((freqs, 2, blocks, points), bf16),
        in_specs=[pl.BlockSpec(memory_space=pltpu.HBM)] * 3,
        out_specs=VMEM,
        scratch_shapes=[
            pltpu.VMEM((2 * freqs * blocks, points), f32),
            pltpu.SMEM(tallies.shape, jnp.int32),
            pltpu.VMEM((1, freqs), jnp.int32),
            pltpu.VMEM(snapshots.shape, bf16),
            pltpu.SemaphoreType.DMA((2 + PARTS,)),
        ],
        compiler_params=pltpu.CompilerParams(vmem_limit_bytes=SMALL),
        name="transform",
    )(
        *[
            pltpu.with_memory_space_constraint(v, pltpu.HBM)
            for v in (tallies, slots.reshape(1, -1), snapshots)
        ]
    )


def places():
    row = lax.axis_index("row")
    x, z = row // SIDE, row % SIDE
    x_first = lax.axis_index("block") % 2 == 0
    return x_first, jnp.where(x_first, x, z), jnp.where(x_first, z, x)


def project_kernel(spectra, modes, *refs):
    outs, acc = refs[:-1], refs[-1]
    x_first, place, _ = places()
    step = jnp.where(x_first, 1, SIDE)
    freqs, points, width = spectra.shape[1], spectra.shape[4], modes.shape[2]
    blocks = spectra.shape[0] * spectra.shape[3]
    for k in range(freqs):
        real = spectra[:, k, 0].reshape(blocks, points)
        imag = spectra[:, k, 1].reshape(blocks, points)
        left = jnp.concatenate(
            [
                jnp.concatenate([real, imag], axis=1),
                jnp.concatenate([imag, -real], axis=1),
            ],
            axis=0,
        )
        slot = k % 2
        acc[slot] = jnp.dot(left, modes[k], preferred_element_type=f32).reshape(acc.shape[1:])
        for i in range(SIDE):
            first = (place + i) % SIDE * jnp.where(x_first, SIDE, 1)
            piece = jnp.stack([acc[slot, :, first + j * step] for j in range(SIDE)], axis=1)
            outs[i][k] = piece.reshape(2, -1, width).astype(outs[i].dtype)


def project(spectra, modes):
    freqs, width = modes.shape[0], modes.shape[2]
    blocks = spectra.shape[0] * spectra.shape[3]
    piece = (freqs, 2, blocks // SIDE, width)
    return pl.pallas_call(
        project_kernel,
        out_shape=[jax.ShapeDtypeStruct(piece, f32 if i == 0 else bf16) for i in range(SIDE)],
        in_specs=[VMEM, VMEM],
        out_specs=[VMEM] * SIDE,
        scratch_shapes=[pltpu.VMEM((2, 2, SIDE * SIDE, blocks // (SIDE * SIDE), width), f32)],
        compiler_params=pltpu.CompilerParams(vmem_limit_bytes=SMALL),
        name="project",
    )(spectra, modes)


def fold_kernel(own, first, second, third, *refs):
    outs, acc = refs[:-1], refs[-1]
    _, _, place = places()
    width = own.shape[3]
    for k in range(own.shape[0]):
        total = own[k] + first[k].astype(f32) + second[k].astype(f32) + third[k].astype(f32)
        acc[k % 2] = total.reshape(acc.shape[1:])
        for i in range(SIDE):
            piece = acc[k % 2, :, (place + i) % SIDE].reshape(-1, width)
            outs[i][k] = piece.astype(outs[i].dtype)


def fold(parts):
    freqs, _, blocks, width = parts[0].shape
    piece = (freqs, 2 * blocks // SIDE, width)
    return pl.pallas_call(
        fold_kernel,
        out_shape=[jax.ShapeDtypeStruct(piece, f32 if i == 0 else bf16) for i in range(SIDE)],
        in_specs=[VMEM] * SIDE,
        out_specs=[VMEM] * SIDE,
        scratch_shapes=[pltpu.VMEM((2, 2, SIDE, blocks // SIDE, width), f32)],
        compiler_params=pltpu.CompilerParams(vmem_limit_bytes=SMALL),
        name="fold",
    )(*parts)


def energy_kernel(tallies, all_tallies, own, first, second, third, energy, own_energy):
    freqs, rows, width = own.shape
    blocks = rows // 2
    start = lax.axis_index("row") * blocks
    total_weight = jnp.sum(all_tallies[...].astype(f32), axis=1, keepdims=True)
    spots = lax.broadcasted_iota(jnp.int32, (rows, width), 0) % blocks
    weights = jnp.zeros((rows, width), f32)
    for j in range(blocks):
        weights = jnp.where(spots == j, tallies[start + j].astype(f32), weights)
    weights = weights / total_weight
    for k in range(freqs):
        total = own[k] + first[k].astype(f32) + second[k].astype(f32) + third[k].astype(f32)
        power = jnp.sum(weights * (total * total), axis=0, keepdims=True)
        own_energy[k : k + 1, :] = power
    energy[...] = jnp.broadcast_to(own_energy[...].astype(bf16)[None], energy.shape)


def coefficients_kernel(own, first, second, third, coefficients):
    blocks = coefficients.shape[0]
    for k in range(own.shape[0]):
        total = own[k] + first[k].astype(f32) + second[k].astype(f32) + third[k].astype(f32)
        coefficients[:, 0, k, :] = total[:blocks]
        coefficients[:, 1, k, :] = total[blocks:]


def sum_kernel(parts, energy):
    energy[...] = jnp.sum(parts[...].astype(f32), axis=0)


def shards(snapshots, usable_frame_tallies, retained_frequency_slots, modes):
    row_width = snapshots.shape[1]
    rows = lax.axis_size("row")
    groups = lax.axis_size("block")
    spectra = transform(usable_frame_tallies, retained_frequency_slots, snapshots)
    spectra = spectra.reshape((groups, -1) + spectra.shape[1:])
    moved = lax.all_to_all(spectra, "block", split_axis=0, concat_axis=0, tiled=True)

    def along(value, stage, distance):
        pairs = []
        for block in range(groups):
            for x in range(SIDE):
                for z in range(SIDE):
                    if (block % 2 == 0) == (stage == 0):
                        target = (x + distance) % SIDE * SIDE + z
                    else:
                        target = x * SIDE + (z + distance) % SIDE
                    pairs.append((block * rows + x * SIDE + z, block * rows + target))
        return lax.ppermute(value, ("block", "row"), pairs)

    mode_rows = modes.reshape(modes.shape[0], 2 * row_width, modes.shape[3])
    pieces = project(moved, mode_rows)
    pieces = fold([pieces[0]] + [along(pieces[i], 0, i) for i in FARTHEST_FIRST])
    last = [pieces[0]] + [along(pieces[i], 1, i) for i in FARTHEST_FIRST]
    freqs, double, width = last[0].shape
    energy_parts = pl.pallas_call(
        energy_kernel,
        out_shape=jax.ShapeDtypeStruct((rows, freqs, width), bf16),
        in_specs=[SMEM] + [VMEM] * (1 + SIDE),
        out_specs=VMEM,
        scratch_shapes=[pltpu.VMEM((freqs, width), f32)],
        compiler_params=pltpu.CompilerParams(vmem_limit_bytes=SMALL),
        name="energy",
    )(usable_frame_tallies, usable_frame_tallies.reshape(1, -1), *last)
    swapped = lax.all_to_all(energy_parts, "row", 0, 0, tiled=True)
    coefficients = pl.pallas_call(
        coefficients_kernel,
        out_shape=jax.ShapeDtypeStruct((double // 2, 2, freqs, width), f32),
        in_specs=[VMEM] * SIDE,
        out_specs=VMEM,
        compiler_params=pltpu.CompilerParams(vmem_limit_bytes=SMALL),
        name="coefficients",
    )(*last)
    energy = pl.pallas_call(
        sum_kernel,
        out_shape=jax.ShapeDtypeStruct((freqs, width), f32),
        in_specs=[VMEM],
        out_specs=VMEM,
        compiler_params=pltpu.CompilerParams(vmem_limit_bytes=SMALL),
        name="total",
    )(swapped)
    return (coefficients, energy)


def solution(mesh):
    placed = (P("block", "row"), P(), P(), P("block", None, "row", None))
    return jax.shard_map(
        shards,
        mesh=mesh,
        in_specs=placed,
        out_specs=(P("row", None, "block", None), P("block", None)),
        check_vma=False,
    )
```

```python
import jax
import jax.numpy as jnp
from jax import lax
from jax.experimental import pallas as pl
from jax.experimental.pallas import tpu as pltpu
from jax.sharding import PartitionSpec as P

FRAMES_PER_SEG = 256
FARTHEST_FIRST = (2, 1, 3)
PARTS = 4
SIDE = 4
VMEM = pl.BlockSpec(memory_space=pltpu.VMEM)
SMEM = pl.BlockSpec(memory_space=pltpu.SMEM)
SMALL = 8 << 20
bf16, f32 = jnp.bfloat16, jnp.float32


def windows(tallies, start, blocks):
    spots = lax.broadcasted_iota(jnp.int32, (blocks, FRAMES_PER_SEG), 0)
    lengths = jnp.zeros((blocks, FRAMES_PER_SEG), jnp.int32)
    for j in range(blocks):
        lengths = jnp.where(spots == j, tallies[start + j], lengths)
    times = lax.broadcasted_iota(jnp.int32, (blocks, FRAMES_PER_SEG), 1)
    angle = jnp.pi * (times.astype(f32) + 0.5) / lengths.astype(f32)
    window = jnp.where(times < lengths, jnp.sin(angle) ** 2, 0.0)
    return window * (1.0 / jnp.sqrt(jnp.sum(window * window, axis=1, keepdims=True)))


def transform_blocks(window, waves, snapshots, acc, arrived):
    blocks, rows = window.shape[0], waves.shape[0]
    for j in range(blocks):
        arrived(j)
        table = (window[j : j + 1] * waves).astype(bf16)
        frames = snapshots[j * FRAMES_PER_SEG : (j + 1) * FRAMES_PER_SEG, :]
        acc[pl.ds(j, rows, stride=blocks), :] = jnp.dot(
            table, frames, preferred_element_type=f32
        )


def own_kernel(
    tallies_hbm, slots_hbm, snapshots_hbm, spectra, waves, other_window,
    acc, tallies, slots, snapshots, sems,
):
    copies = [
        pltpu.make_async_copy(tallies_hbm, tallies, sems.at[0]),
        pltpu.make_async_copy(slots_hbm, slots, sems.at[1]),
    ]
    share = snapshots.shape[0] // PARTS
    for part in range(PARTS):
        rows = pl.ds(part * share, share)
        copies.append(
            pltpu.make_async_copy(
                snapshots_hbm.at[rows, :], snapshots.at[rows, :], sems.at[2 + part]
            )
        )
    for copy in copies:
        copy.start()
    copies[0].wait()
    copies[1].wait()
    block = lax.axis_index("block")
    core = block % 2
    blocks = other_window.shape[0]
    window = windows(tallies, block * blocks, blocks)
    other_window[...] = windows(tallies, (block + 1 - 2 * core) * blocks, blocks)
    times = lax.broadcasted_iota(jnp.int32, (1, FRAMES_PER_SEG), 1)
    turns = lax.dot_general(
        slots[...].astype(f32).astype(bf16),
        times.astype(f32).astype(bf16),
        (((0,), (0,)), ((), ())),
        preferred_element_type=f32,
    )
    turns = turns.reshape(SIDE, 2, -1, FRAMES_PER_SEG)
    turns = jnp.where(core == 0, turns[:, 0], turns[:, 1]).reshape(-1, FRAMES_PER_SEG)
    turns = (turns.astype(jnp.int32) % FRAMES_PER_SEG).astype(f32)
    phase = turns * (2.0 * jnp.pi / FRAMES_PER_SEG)
    waves[...] = jnp.concatenate([jnp.cos(phase), -jnp.sin(phase)], axis=0)

    def arrived(j):
        if j % (blocks // PARTS) == 0:
            copies[2 + j // (blocks // PARTS)].wait()

    transform_blocks(window, waves[...], snapshots, acc, arrived)
    spectra[...] = acc[...].astype(bf16).reshape(spectra.shape)


def other_kernel(own, waves, window, snapshots, *refs):
    outs, acc = refs[:-1], refs[-1]
    block = lax.axis_index("block")
    y, core = block // 2, block % 2
    transform_blocks(window[...], waves[...], snapshots, acc, lambda j: None)
    _, _, freqs, blocks, points = own.shape
    size = freqs * blocks
    for i in range(SIDE):
        target = (y + i) % SIDE
        for c in range(2):
            rows = pl.ds(pl.multiple_of((c * SIDE + target) * size, size), size)
            outs[i][:, c, core] = own[c, target]
            outs[i][:, c, 1 - core] = acc[rows, :].astype(bf16).reshape(freqs, blocks, points)


def transform(tallies, slots, snapshots):
    blocks, points = snapshots.shape[0] // FRAMES_PER_SEG, snapshots.shape[1]
    freqs = slots.shape[0] // (2 * SIDE)
    rows = 2 * SIDE * freqs
    swap = [(b, b ^ 1) for b in range(lax.axis_size("block"))]
    others = lax.ppermute(snapshots, "block", swap)
    own, waves, window = pl.pallas_call(
        own_kernel,
        out_shape=[
            jax.ShapeDtypeStruct((2, SIDE, freqs, blocks, points), bf16),
            jax.ShapeDtypeStruct((rows, FRAMES_PER_SEG), f32),
            jax.ShapeDtypeStruct((blocks, FRAMES_PER_SEG), f32),
        ],
        in_specs=[pl.BlockSpec(memory_space=pltpu.HBM)] * 3,
        out_specs=[VMEM] * 3,
        scratch_shapes=[
            pltpu.VMEM((rows * blocks, points), f32),
            pltpu.SMEM(tallies.shape, jnp.int32),
            pltpu.VMEM((1, slots.shape[0]), jnp.int32),
            pltpu.VMEM(snapshots.shape, bf16),
            pltpu.SemaphoreType.DMA((2 + PARTS,)),
        ],
        compiler_params=pltpu.CompilerParams(vmem_limit_bytes=SMALL),
        name="transform_own",
    )(
        *[
            pltpu.with_memory_space_constraint(v, pltpu.HBM)
            for v in (tallies, slots.reshape(1, -1), snapshots)
        ]
    )
    return pl.pallas_call(
        other_kernel,
        out_shape=[jax.ShapeDtypeStruct((freqs, 2, 2, blocks, points), bf16)] * SIDE,
        in_specs=[VMEM] * 4,
        out_specs=[VMEM] * SIDE,
        scratch_shapes=[pltpu.VMEM((rows * blocks, points), f32)],
        compiler_params=pltpu.CompilerParams(vmem_limit_bytes=SMALL),
        name="transform_other",
    )(own, waves, window, others)


def places():
    row = lax.axis_index("row")
    x, z = row // SIDE, row % SIDE
    x_first = lax.axis_index("block") % 2 == 0
    return x_first, jnp.where(x_first, x, z), jnp.where(x_first, z, x)


def project_kernel(*refs):
    spectra, modes, outs, acc = refs[:SIDE], refs[SIDE], refs[SIDE + 1 : -1], refs[-1]
    x_first, place, _ = places()
    y = lax.axis_index("block") // 2
    freqs, points, width = spectra[0].shape[0], spectra[0].shape[4], modes.shape[2]
    for k in range(freqs):
        real, imag = (
            jnp.concatenate([part[k, c].reshape(-1, points) for part in spectra], axis=0)
            for c in range(2)
        )
        left = jnp.concatenate(
            [
                jnp.concatenate([real, imag], axis=1),
                jnp.concatenate([imag, -real], axis=1),
            ],
            axis=0,
        )
        slot = k % 2
        acc[slot] = jnp.dot(left, modes[k], preferred_element_type=f32).reshape(acc.shape[1:])
        for i in range(SIDE):
            target = (place + i) % SIDE
            piece = []
            for j in range(SIDE):
                x = jnp.where(x_first, target, j)
                z = jnp.where(x_first, j, target)
                piece.append(acc[slot, :, (y + SIDE - x) % SIDE * SIDE + z])
            piece = jnp.stack(piece, axis=1)
            outs[i][k] = piece.reshape(2, -1, width).astype(outs[i].dtype)


def project(spectra, modes):
    freqs, width = modes.shape[0], modes.shape[2]
    blocks = SIDE * spectra[0].shape[2] * spectra[0].shape[3]
    piece = (freqs, 2, blocks // SIDE, width)
    return pl.pallas_call(
        project_kernel,
        out_shape=[jax.ShapeDtypeStruct(piece, f32 if i == 0 else bf16) for i in range(SIDE)],
        in_specs=[VMEM] * (SIDE + 1),
        out_specs=[VMEM] * SIDE,
        scratch_shapes=[pltpu.VMEM((2, 2, SIDE * SIDE, blocks // (SIDE * SIDE), width), f32)],
        compiler_params=pltpu.CompilerParams(vmem_limit_bytes=SMALL),
        name="project",
    )(*spectra, modes)


def fold_kernel(own, first, second, third, *refs):
    outs, acc = refs[:-1], refs[-1]
    _, _, place = places()
    width = own.shape[3]
    for k in range(own.shape[0]):
        total = own[k] + first[k].astype(f32) + second[k].astype(f32) + third[k].astype(f32)
        acc[k % 2] = total.reshape(acc.shape[1:])
        for i in range(SIDE):
            piece = acc[k % 2, :, (place + i) % SIDE].reshape(-1, width)
            outs[i][k] = piece.astype(outs[i].dtype)


def fold(parts):
    freqs, _, blocks, width = parts[0].shape
    piece = (freqs, 2 * blocks // SIDE, width)
    return pl.pallas_call(
        fold_kernel,
        out_shape=[jax.ShapeDtypeStruct(piece, f32 if i == 0 else bf16) for i in range(SIDE)],
        in_specs=[VMEM] * SIDE,
        out_specs=[VMEM] * SIDE,
        scratch_shapes=[pltpu.VMEM((2, 2, SIDE, blocks // SIDE, width), f32)],
        compiler_params=pltpu.CompilerParams(vmem_limit_bytes=SMALL),
        name="fold",
    )(*parts)


def energy_kernel(tallies, all_tallies, own, first, second, third, energy, own_energy):
    freqs, rows, width = own.shape
    blocks = rows // 2
    start = lax.axis_index("row") * blocks
    total_weight = jnp.sum(all_tallies[...].astype(f32), axis=1, keepdims=True)
    spots = lax.broadcasted_iota(jnp.int32, (rows, width), 0) % blocks
    weights = jnp.zeros((rows, width), f32)
    for j in range(blocks):
        weights = jnp.where(spots == j, tallies[start + j].astype(f32), weights)
    weights = weights / total_weight
    for k in range(freqs):
        total = own[k] + first[k].astype(f32) + second[k].astype(f32) + third[k].astype(f32)
        power = jnp.sum(weights * (total * total), axis=0, keepdims=True)
        own_energy[k : k + 1, :] = power
    energy[...] = jnp.broadcast_to(own_energy[...].astype(bf16)[None], energy.shape)


def coefficients_kernel(own, first, second, third, coefficients):
    blocks = coefficients.shape[0]
    for k in range(own.shape[0]):
        total = own[k] + first[k].astype(f32) + second[k].astype(f32) + third[k].astype(f32)
        coefficients[:, 0, k, :] = total[:blocks]
        coefficients[:, 1, k, :] = total[blocks:]


def sum_kernel(parts, energy):
    energy[...] = jnp.sum(parts[...].astype(f32), axis=0)


def shards(snapshots, usable_frame_tallies, retained_frequency_slots, modes):
    row_width = snapshots.shape[1]
    rows = lax.axis_size("row")
    groups = lax.axis_size("block")
    spectra = transform(usable_frame_tallies, retained_frequency_slots, snapshots)

    def along_y(value, distance):
        pairs = [(b, (b + 2 * distance) % groups) for b in range(groups)]
        return lax.ppermute(value, "block", pairs)

    moved = {0: spectra[0]}
    for i in FARTHEST_FIRST:
        moved[i] = along_y(spectra[i], i)

    def along(value, stage, distance):
        pairs = []
        for block in range(groups):
            for x in range(SIDE):
                for z in range(SIDE):
                    if (block % 2 == 0) == (stage == 0):
                        target = (x + distance) % SIDE * SIDE + z
                    else:
                        target = x * SIDE + (z + distance) % SIDE
                    pairs.append((block * rows + x * SIDE + z, block * rows + target))
        return lax.ppermute(value, ("block", "row"), pairs)

    mode_rows = modes.reshape(modes.shape[0], 2 * row_width, modes.shape[3])
    pieces = project([moved[i] for i in range(SIDE)], mode_rows)
    pieces = fold([pieces[0]] + [along(pieces[i], 0, i) for i in FARTHEST_FIRST])
    last = [pieces[0]] + [along(pieces[i], 1, i) for i in FARTHEST_FIRST]
    freqs, double, width = last[0].shape
    energy_parts = pl.pallas_call(
        energy_kernel,
        out_shape=jax.ShapeDtypeStruct((rows, freqs, width), bf16),
        in_specs=[SMEM] + [VMEM] * (1 + SIDE),
        out_specs=VMEM,
        scratch_shapes=[pltpu.VMEM((freqs, width), f32)],
        compiler_params=pltpu.CompilerParams(vmem_limit_bytes=SMALL),
        name="energy",
    )(usable_frame_tallies, usable_frame_tallies.reshape(1, -1), *last)
    swapped = lax.all_to_all(energy_parts, "row", 0, 0, tiled=True)
    coefficients = pl.pallas_call(
        coefficients_kernel,
        out_shape=jax.ShapeDtypeStruct((double // 2, 2, freqs, width), f32),
        in_specs=[VMEM] * SIDE,
        out_specs=VMEM,
        compiler_params=pltpu.CompilerParams(vmem_limit_bytes=SMALL),
        name="coefficients",
    )(*last)
    energy = pl.pallas_call(
        sum_kernel,
        out_shape=jax.ShapeDtypeStruct((freqs, width), f32),
        in_specs=[VMEM],
        out_specs=VMEM,
        compiler_params=pltpu.CompilerParams(vmem_limit_bytes=SMALL),
        name="total",
    )(swapped)
    return (coefficients, energy)


def solution(mesh):
    placed = (P("block", "row"), P(), P(), P("block", None, "row", None))
    return jax.shard_map(
        shards,
        mesh=mesh,
        in_specs=placed,
        out_specs=(P("row", None, "block", None), P("block", None)),
        check_vma=False,
    )
```

```python
import jax
import jax.numpy as jnp
from jax import lax
from jax.experimental import pallas as pl
from jax.experimental.pallas import tpu as pltpu
from jax.sharding import PartitionSpec as P

FRAMES_PER_SEG = 256
FARTHEST_FIRST = (2, 1, 3)
PARTS = 4
SIDE = 4
VMEM = pl.BlockSpec(memory_space=pltpu.VMEM)
SMEM = pl.BlockSpec(memory_space=pltpu.SMEM)
SMALL = 8 << 20
bf16, f32 = jnp.bfloat16, jnp.float32


def windows(tallies, start, blocks):
    spots = lax.broadcasted_iota(jnp.int32, (blocks, FRAMES_PER_SEG), 0)
    lengths = jnp.zeros((blocks, FRAMES_PER_SEG), jnp.int32)
    for j in range(blocks):
        lengths = jnp.where(spots == j, tallies[start + j], lengths)
    times = lax.broadcasted_iota(jnp.int32, (blocks, FRAMES_PER_SEG), 1)
    angle = jnp.pi * (times.astype(f32) + 0.5) / lengths.astype(f32)
    window = jnp.where(times < lengths, jnp.sin(angle) ** 2, 0.0)
    return window * (1.0 / jnp.sqrt(jnp.sum(window * window, axis=1, keepdims=True)))


def transform_blocks(window, waves, snapshots, acc, arrived):
    blocks, rows = window.shape[0], waves.shape[0]
    for j in range(blocks):
        arrived(j)
        table = (window[j : j + 1] * waves).astype(bf16)
        frames = snapshots[j * FRAMES_PER_SEG : (j + 1) * FRAMES_PER_SEG, :]
        acc[pl.ds(j, rows, stride=blocks), :] = jnp.dot(
            table, frames, preferred_element_type=f32
        )


def own_kernel(
    tallies_hbm, slots_hbm, snapshots_hbm, spectra, waves, other_window,
    acc, tallies, slots, snapshots, sems,
):
    copies = [
        pltpu.make_async_copy(tallies_hbm, tallies, sems.at[0]),
        pltpu.make_async_copy(slots_hbm, slots, sems.at[1]),
    ]
    share = snapshots.shape[0] // PARTS
    for part in range(PARTS):
        rows = pl.ds(part * share, share)
        copies.append(
            pltpu.make_async_copy(
                snapshots_hbm.at[rows, :], snapshots.at[rows, :], sems.at[2 + part]
            )
        )
    for copy in copies:
        copy.start()
    copies[0].wait()
    copies[1].wait()
    block = lax.axis_index("block")
    core = block % 2
    blocks = other_window.shape[0]
    window = windows(tallies, block * blocks, blocks)
    other_window[...] = windows(tallies, (block + 1 - 2 * core) * blocks, blocks)
    times = lax.broadcasted_iota(jnp.int32, (1, FRAMES_PER_SEG), 1)
    turns = lax.dot_general(
        slots[...].astype(f32).astype(bf16),
        times.astype(f32).astype(bf16),
        (((0,), (0,)), ((), ())),
        preferred_element_type=f32,
    )
    turns = turns.reshape(SIDE, 2, -1, FRAMES_PER_SEG)
    turns = jnp.where(core == 0, turns[:, 0], turns[:, 1]).reshape(-1, FRAMES_PER_SEG)
    turns = (turns.astype(jnp.int32) % FRAMES_PER_SEG).astype(f32)
    phase = turns * (2.0 * jnp.pi / FRAMES_PER_SEG)
    waves[...] = jnp.concatenate([jnp.cos(phase), -jnp.sin(phase)], axis=0)

    def arrived(j):
        if j % (blocks // PARTS) == 0:
            copies[2 + j // (blocks // PARTS)].wait()

    transform_blocks(window, waves[...], snapshots, acc, arrived)
    spectra[...] = acc[...].astype(bf16).reshape(spectra.shape)


def other_kernel(own, waves, window, snapshots, *refs):
    outs, acc = refs[:-1], refs[-1]
    block = lax.axis_index("block")
    y, core = block // 2, block % 2
    transform_blocks(window[...], waves[...], snapshots, acc, lambda j: None)
    _, _, freqs, blocks, points = own.shape
    size = freqs * blocks
    for i in range(SIDE):
        target = (y + i) % SIDE
        for c in range(2):
            rows = pl.ds(pl.multiple_of((c * SIDE + target) * size, size), size)
            outs[i][:, c, core] = own[c, target]
            outs[i][:, c, 1 - core] = acc[rows, :].astype(bf16).reshape(freqs, blocks, points)


def transform(tallies, slots, snapshots):
    blocks, points = snapshots.shape[0] // FRAMES_PER_SEG, snapshots.shape[1]
    freqs = slots.shape[0] // (2 * SIDE)
    rows = 2 * SIDE * freqs
    swap = [(b, b ^ 1) for b in range(lax.axis_size("block"))]
    others = lax.ppermute(snapshots, "block", swap)
    own, waves, window = pl.pallas_call(
        own_kernel,
        out_shape=[
            jax.ShapeDtypeStruct((2, SIDE, freqs, blocks, points), bf16),
            jax.ShapeDtypeStruct((rows, FRAMES_PER_SEG), f32),
            jax.ShapeDtypeStruct((blocks, FRAMES_PER_SEG), f32),
        ],
        in_specs=[pl.BlockSpec(memory_space=pltpu.HBM)] * 3,
        out_specs=[VMEM] * 3,
        scratch_shapes=[
            pltpu.VMEM((rows * blocks, points), f32),
            pltpu.SMEM(tallies.shape, jnp.int32),
            pltpu.VMEM((1, slots.shape[0]), jnp.int32),
            pltpu.VMEM(snapshots.shape, bf16),
            pltpu.SemaphoreType.DMA((2 + PARTS,)),
        ],
        compiler_params=pltpu.CompilerParams(vmem_limit_bytes=SMALL),
        name="transform_own",
    )(
        *[
            pltpu.with_memory_space_constraint(v, pltpu.HBM)
            for v in (tallies, slots.reshape(1, -1), snapshots)
        ]
    )
    return pl.pallas_call(
        other_kernel,
        out_shape=[jax.ShapeDtypeStruct((freqs, 2, 2, blocks, points), bf16)] * SIDE,
        in_specs=[VMEM] * 4,
        out_specs=[VMEM] * SIDE,
        scratch_shapes=[pltpu.VMEM((rows * blocks, points), f32)],
        compiler_params=pltpu.CompilerParams(vmem_limit_bytes=SMALL),
        name="transform_other",
    )(own, waves, window, others)


def places():
    row = lax.axis_index("row")
    x, z = row // SIDE, row % SIDE
    x_first = lax.axis_index("block") % 2 == 0
    return x_first, jnp.where(x_first, x, z), jnp.where(x_first, z, x)


def project_kernel(*refs):
    spectra, modes, outs, acc = refs[:SIDE], refs[SIDE], refs[SIDE + 1 : -1], refs[-1]
    x_first, place, _ = places()
    y = lax.axis_index("block") // 2
    freqs, points, width = spectra[0].shape[0], spectra[0].shape[4], modes.shape[2]
    for k in range(freqs):
        real, imag = (
            jnp.concatenate([part[k, c].reshape(-1, points) for part in spectra], axis=0)
            for c in range(2)
        )
        left = jnp.concatenate(
            [
                jnp.concatenate([real, imag], axis=1),
                jnp.concatenate([imag, -real], axis=1),
            ],
            axis=0,
        )
        slot = k % 2
        acc[slot] = jnp.dot(left, modes[k], preferred_element_type=f32).reshape(acc.shape[1:])
        half = k // (freqs // 2)
        for i, flip in enumerate((0, 3 - 2 * half, 1 + 2 * half, 2)):
            target = place ^ flip
            piece = []
            for j in range(SIDE):
                x = jnp.where(x_first, target, j)
                z = jnp.where(x_first, j, target)
                piece.append(acc[slot, :, (y + SIDE - x) % SIDE * SIDE + z])
            piece = jnp.stack(piece, axis=1)
            out = outs[half * SIDE + i]
            out[k % (freqs // 2)] = piece.reshape(2, -1, width).astype(out.dtype)


def project(spectra, modes):
    freqs, width = modes.shape[0], modes.shape[2]
    blocks = SIDE * spectra[0].shape[2] * spectra[0].shape[3]
    piece = (freqs // 2, 2, blocks // SIDE, width)
    return pl.pallas_call(
        project_kernel,
        out_shape=[jax.ShapeDtypeStruct(piece, t) for t in (f32, f32, bf16, bf16) * 2],
        in_specs=[VMEM] * (SIDE + 1),
        out_specs=[VMEM] * (2 * SIDE),
        scratch_shapes=[pltpu.VMEM((2, 2, SIDE * SIDE, blocks // (SIDE * SIDE), width), f32)],
        compiler_params=pltpu.CompilerParams(vmem_limit_bytes=SMALL),
        name="project",
    )(*spectra, modes)


def relay_kernel(held, came, out):
    out[...] = (held[...] + came[...].astype(f32)).astype(bf16)


def relay(held, came):
    return pl.pallas_call(
        relay_kernel,
        out_shape=jax.ShapeDtypeStruct(came.shape, bf16),
        in_specs=[VMEM] * 2,
        out_specs=VMEM,
        compiler_params=pltpu.CompilerParams(vmem_limit_bytes=SMALL),
        name="relay",
    )(held, came)


def fold_kernel(*refs):
    parts, outs, acc = refs[:6], refs[6:-1], refs[-1]
    _, _, place = places()
    half, width = parts[0].shape[0], parts[0].shape[3]
    for k in range(2 * half):
        own, direct, relayed = parts[3 * (k // half) : 3 * (k // half) + 3]
        total = own[k % half] + direct[k % half].astype(f32) + relayed[k % half].astype(f32)
        acc[k % 2] = total.reshape(acc.shape[1:])
        for i in range(SIDE):
            piece = acc[k % 2, :, (place + i) % SIDE].reshape(-1, width)
            outs[i][k] = piece.astype(outs[i].dtype)


def fold(parts):
    half, _, blocks, width = parts[0].shape
    piece = (2 * half, 2 * blocks // SIDE, width)
    return pl.pallas_call(
        fold_kernel,
        out_shape=[jax.ShapeDtypeStruct(piece, f32 if i == 0 else bf16) for i in range(SIDE)],
        in_specs=[VMEM] * 6,
        out_specs=[VMEM] * SIDE,
        scratch_shapes=[pltpu.VMEM((2, 2, SIDE, blocks // SIDE, width), f32)],
        compiler_params=pltpu.CompilerParams(vmem_limit_bytes=SMALL),
        name="fold",
    )(*parts)


def energy_kernel(tallies, all_tallies, own, first, second, third, energy, own_energy):
    freqs, rows, width = own.shape
    blocks = rows // 2
    start = lax.axis_index("row") * blocks
    total_weight = jnp.sum(all_tallies[...].astype(f32), axis=1, keepdims=True)
    spots = lax.broadcasted_iota(jnp.int32, (rows, width), 0) % blocks
    weights = jnp.zeros((rows, width), f32)
    for j in range(blocks):
        weights = jnp.where(spots == j, tallies[start + j].astype(f32), weights)
    weights = weights / total_weight
    for k in range(freqs):
        total = own[k] + first[k].astype(f32) + second[k].astype(f32) + third[k].astype(f32)
        power = jnp.sum(weights * (total * total), axis=0, keepdims=True)
        own_energy[k : k + 1, :] = power
    energy[...] = jnp.broadcast_to(own_energy[...].astype(bf16)[None], energy.shape)


def coefficients_kernel(own, first, second, third, coefficients):
    blocks = coefficients.shape[0]
    for k in range(own.shape[0]):
        total = own[k] + first[k].astype(f32) + second[k].astype(f32) + third[k].astype(f32)
        coefficients[:, 0, k, :] = total[:blocks]
        coefficients[:, 1, k, :] = total[blocks:]


def sum_kernel(parts, energy):
    energy[...] = jnp.sum(parts[...].astype(f32), axis=0)


def shards(snapshots, usable_frame_tallies, retained_frequency_slots, modes):
    row_width = snapshots.shape[1]
    rows = lax.axis_size("row")
    groups = lax.axis_size("block")
    spectra = transform(usable_frame_tallies, retained_frequency_slots, snapshots)

    def along_y(value, distance):
        pairs = [(b, (b + 2 * distance) % groups) for b in range(groups)]
        return lax.ppermute(value, "block", pairs)

    moved = {0: spectra[0]}
    for i in FARTHEST_FIRST:
        moved[i] = along_y(spectra[i], i)

    def along(value, stage, move):
        pairs = []
        for block in range(groups):
            for x in range(SIDE):
                for z in range(SIDE):
                    if (block % 2 == 0) == (stage == 0):
                        target = move(x) * SIDE + z
                    else:
                        target = x * SIDE + move(z)
                    pairs.append((block * rows + x * SIDE + z, block * rows + target))
        return lax.ppermute(value, ("block", "row"), pairs)

    def flipped(value, bits):
        return along(value, 0, lambda place: place ^ bits)

    def onward(value, distance):
        return along(value, 1, lambda place: (place + distance) % SIDE)

    mode_rows = modes.reshape(modes.shape[0], 2 * row_width, modes.shape[3])
    pieces = project([moved[i] for i in range(SIDE)], mode_rows)
    own_a, held_a, direct_a, far_a, own_b, held_b, direct_b, far_b = pieces
    far_a, far_b = flipped(far_a, 1), flipped(far_b, 3)
    direct_a, direct_b = flipped(direct_a, 1), flipped(direct_b, 3)
    relayed_a = flipped(relay(held_a, far_a), 3)
    relayed_b = flipped(relay(held_b, far_b), 1)
    pieces = fold([own_a, direct_a, relayed_a, own_b, direct_b, relayed_b])
    came = {i: onward(pieces[i], i) for i in (1, 3, 2)}
    last = [pieces[0]] + [came[i] for i in range(1, SIDE)]
    freqs, double, width = last[0].shape
    energy_parts = pl.pallas_call(
        energy_kernel,
        out_shape=jax.ShapeDtypeStruct((rows, freqs, width), bf16),
        in_specs=[SMEM] + [VMEM] * (1 + SIDE),
        out_specs=VMEM,
        scratch_shapes=[pltpu.VMEM((freqs, width), f32)],
        compiler_params=pltpu.CompilerParams(vmem_limit_bytes=SMALL),
        name="energy",
    )(usable_frame_tallies, usable_frame_tallies.reshape(1, -1), *last)
    swapped = lax.all_to_all(energy_parts, "row", 0, 0, tiled=True)
    coefficients = pl.pallas_call(
        coefficients_kernel,
        out_shape=jax.ShapeDtypeStruct((double // 2, 2, freqs, width), f32),
        in_specs=[VMEM] * SIDE,
        out_specs=VMEM,
        compiler_params=pltpu.CompilerParams(vmem_limit_bytes=SMALL),
        name="coefficients",
    )(*last)
    energy = pl.pallas_call(
        sum_kernel,
        out_shape=jax.ShapeDtypeStruct((freqs, width), f32),
        in_specs=[VMEM],
        out_specs=VMEM,
        compiler_params=pltpu.CompilerParams(vmem_limit_bytes=SMALL),
        name="total",
    )(swapped)
    return (coefficients, energy)


def solution(mesh):
    placed = (P("block", "row"), P(), P(), P("block", None, "row", None))
    return jax.shard_map(
        shards,
        mesh=mesh,
        in_specs=placed,
        out_specs=(P("row", None, "block", None), P("block", None)),
        check_vma=False,
    )
```

```python
import jax
import jax.numpy as jnp
from jax import lax
from jax.experimental import pallas as pl
from jax.experimental.pallas import tpu as pltpu
from jax.sharding import PartitionSpec as P

FRAMES_PER_SEG = 256
FARTHEST_FIRST = (2, 1, 3)
PARTS = 4
SIDE = 4
VMEM = pl.BlockSpec(memory_space=pltpu.VMEM)
SMEM = pl.BlockSpec(memory_space=pltpu.SMEM)
SMALL = 8 << 20
bf16, f32 = jnp.bfloat16, jnp.float32


def windows(tallies, start, blocks):
    spots = lax.broadcasted_iota(jnp.int32, (blocks, FRAMES_PER_SEG), 0)
    lengths = jnp.zeros((blocks, FRAMES_PER_SEG), jnp.int32)
    for j in range(blocks):
        lengths = jnp.where(spots == j, tallies[start + j], lengths)
    times = lax.broadcasted_iota(jnp.int32, (blocks, FRAMES_PER_SEG), 1)
    angle = jnp.pi * (times.astype(f32) + 0.5) / lengths.astype(f32)
    window = jnp.where(times < lengths, jnp.sin(angle) ** 2, 0.0)
    return window * (1.0 / jnp.sqrt(jnp.sum(window * window, axis=1, keepdims=True)))


def transform_blocks(window, waves, snapshots, acc, arrived):
    blocks, rows = window.shape[0], waves.shape[0]
    for j in range(blocks):
        arrived(j)
        table = (window[j : j + 1] * waves).astype(bf16)
        frames = snapshots[j * FRAMES_PER_SEG : (j + 1) * FRAMES_PER_SEG, :]
        acc[pl.ds(j, rows, stride=blocks), :] = jnp.dot(
            table, frames, preferred_element_type=f32
        )


def own_kernel(
    tallies_hbm, slots_hbm, snapshots_hbm, spectra, waves, other_window,
    acc, tallies, slots, snapshots, sems,
):
    copies = [
        pltpu.make_async_copy(tallies_hbm, tallies, sems.at[0]),
        pltpu.make_async_copy(slots_hbm, slots, sems.at[1]),
    ]
    share = snapshots.shape[0] // PARTS
    for part in range(PARTS):
        rows = pl.ds(part * share, share)
        copies.append(
            pltpu.make_async_copy(
                snapshots_hbm.at[rows, :], snapshots.at[rows, :], sems.at[2 + part]
            )
        )
    for copy in copies:
        copy.start()
    copies[0].wait()
    copies[1].wait()
    block = lax.axis_index("block")
    core = block % 2
    blocks = other_window.shape[0]
    window = windows(tallies, block * blocks, blocks)
    other_window[...] = windows(tallies, (block + 1 - 2 * core) * blocks, blocks)
    times = lax.broadcasted_iota(jnp.int32, (1, FRAMES_PER_SEG), 1)
    turns = lax.dot_general(
        slots[...].astype(f32).astype(bf16),
        times.astype(f32).astype(bf16),
        (((0,), (0,)), ((), ())),
        preferred_element_type=f32,
    )
    turns = turns.reshape(SIDE, 2, -1, FRAMES_PER_SEG)
    turns = jnp.where(core == 0, turns[:, 0], turns[:, 1]).reshape(-1, FRAMES_PER_SEG)
    turns = (turns.astype(jnp.int32) % FRAMES_PER_SEG).astype(f32)
    phase = turns * (2.0 * jnp.pi / FRAMES_PER_SEG)
    waves[...] = jnp.concatenate([jnp.cos(phase), -jnp.sin(phase)], axis=0)

    def arrived(j):
        if j % (blocks // PARTS) == 0:
            copies[2 + j // (blocks // PARTS)].wait()

    transform_blocks(window, waves[...], snapshots, acc, arrived)
    spectra[...] = acc[...].astype(bf16).reshape(spectra.shape)


def other_kernel(own, waves, window, snapshots, *refs):
    outs, acc = refs[:-1], refs[-1]
    block = lax.axis_index("block")
    y, core = block // 2, block % 2
    transform_blocks(window[...], waves[...], snapshots, acc, lambda j: None)
    _, _, freqs, blocks, points = own.shape
    size = freqs * blocks
    for i in range(SIDE):
        target = (y + i) % SIDE
        for c in range(2):
            rows = pl.ds(pl.multiple_of((c * SIDE + target) * size, size), size)
            outs[i][:, c, core] = own[c, target]
            outs[i][:, c, 1 - core] = acc[rows, :].astype(bf16).reshape(freqs, blocks, points)


def transform(tallies, slots, snapshots):
    blocks, points = snapshots.shape[0] // FRAMES_PER_SEG, snapshots.shape[1]
    freqs = slots.shape[0] // (2 * SIDE)
    rows = 2 * SIDE * freqs
    swap = [(b, b ^ 1) for b in range(lax.axis_size("block"))]
    others = lax.ppermute(snapshots, "block", swap)
    own, waves, window = pl.pallas_call(
        own_kernel,
        out_shape=[
            jax.ShapeDtypeStruct((2, SIDE, freqs, blocks, points), bf16),
            jax.ShapeDtypeStruct((rows, FRAMES_PER_SEG), f32),
            jax.ShapeDtypeStruct((blocks, FRAMES_PER_SEG), f32),
        ],
        in_specs=[pl.BlockSpec(memory_space=pltpu.HBM)] * 3,
        out_specs=[VMEM] * 3,
        scratch_shapes=[
            pltpu.VMEM((rows * blocks, points), f32),
            pltpu.SMEM(tallies.shape, jnp.int32),
            pltpu.VMEM((1, slots.shape[0]), jnp.int32),
            pltpu.VMEM(snapshots.shape, bf16),
            pltpu.SemaphoreType.DMA((2 + PARTS,)),
        ],
        compiler_params=pltpu.CompilerParams(vmem_limit_bytes=SMALL),
        name="transform_own",
    )(
        *[
            pltpu.with_memory_space_constraint(v, pltpu.HBM)
            for v in (tallies, slots.reshape(1, -1), snapshots)
        ]
    )
    return pl.pallas_call(
        other_kernel,
        out_shape=[jax.ShapeDtypeStruct((freqs, 2, 2, blocks, points), bf16)] * SIDE,
        in_specs=[VMEM] * 4,
        out_specs=[VMEM] * SIDE,
        scratch_shapes=[pltpu.VMEM((rows * blocks, points), f32)],
        compiler_params=pltpu.CompilerParams(vmem_limit_bytes=SMALL),
        name="transform_other",
    )(own, waves, window, others)


def places():
    row = lax.axis_index("row")
    x, z = row // SIDE, row % SIDE
    x_first = lax.axis_index("block") % 2 == 1
    return x_first, jnp.where(x_first, x, z), jnp.where(x_first, z, x)


def project_kernel(*refs):
    spectra, modes, outs, acc = refs[:SIDE], refs[SIDE], refs[SIDE + 1 : -1], refs[-1]
    x_first, place, _ = places()
    y = lax.axis_index("block") // 2
    freqs, points, width = spectra[0].shape[0], spectra[0].shape[4], modes.shape[2]
    for k in range(freqs):
        real, imag = (
            jnp.concatenate([part[k, c].reshape(-1, points) for part in spectra], axis=0)
            for c in range(2)
        )
        left = jnp.concatenate(
            [
                jnp.concatenate([real, imag], axis=1),
                jnp.concatenate([imag, -real], axis=1),
            ],
            axis=0,
        )
        slot = k % 2
        acc[slot] = jnp.dot(left, modes[k], preferred_element_type=f32).reshape(acc.shape[1:])
        half = k // (freqs // 2)
        for i, flip in enumerate((0, 3 - 2 * half, 1 + 2 * half, 2)):
            target = place ^ flip
            piece = []
            for j in range(SIDE):
                x = jnp.where(x_first, target, j)
                z = jnp.where(x_first, j, target)
                piece.append(acc[slot, :, (y + SIDE - x) % SIDE * SIDE + z])
            piece = jnp.stack(piece, axis=1)
            out = outs[half * SIDE + i]
            out[k % (freqs // 2)] = piece.reshape(2, -1, width).astype(out.dtype)


def project(spectra, modes):
    freqs, width = modes.shape[0], modes.shape[2]
    blocks = SIDE * spectra[0].shape[2] * spectra[0].shape[3]
    piece = (freqs // 2, 2, blocks // SIDE, width)
    return pl.pallas_call(
        project_kernel,
        out_shape=[jax.ShapeDtypeStruct(piece, t) for t in (f32, f32, bf16, bf16) * 2],
        in_specs=[VMEM] * (SIDE + 1),
        out_specs=[VMEM] * (2 * SIDE),
        scratch_shapes=[pltpu.VMEM((2, 2, SIDE * SIDE, blocks // (SIDE * SIDE), width), f32)],
        compiler_params=pltpu.CompilerParams(vmem_limit_bytes=SMALL),
        name="project",
    )(*spectra, modes)


def relay_kernel(held, came, out):
    out[...] = (held[...] + came[...].astype(f32)).astype(bf16)


def relay(held, came):
    return pl.pallas_call(
        relay_kernel,
        out_shape=jax.ShapeDtypeStruct(came.shape, bf16),
        in_specs=[VMEM] * 2,
        out_specs=VMEM,
        compiler_params=pltpu.CompilerParams(vmem_limit_bytes=SMALL),
        name="relay",
    )(held, came)


def fold_kernel(*refs):
    parts, outs, acc = refs[:6], refs[6:-1], refs[-1]
    _, _, place = places()
    half, width = parts[0].shape[0], parts[0].shape[3]
    for k in range(2 * half):
        own, direct, relayed = parts[3 * (k // half) : 3 * (k // half) + 3]
        total = own[k % half] + direct[k % half].astype(f32) + relayed[k % half].astype(f32)
        acc[k % 2] = total.reshape(acc.shape[1:])
        for i in range(SIDE):
            piece = acc[k % 2, :, (place + i) % SIDE].reshape(-1, width)
            outs[i][k] = piece.astype(outs[i].dtype)


def fold(parts):
    half, _, blocks, width = parts[0].shape
    piece = (2 * half, 2 * blocks // SIDE, width)
    return pl.pallas_call(
        fold_kernel,
        out_shape=[jax.ShapeDtypeStruct(piece, f32 if i == 0 else bf16) for i in range(SIDE)],
        in_specs=[VMEM] * 6,
        out_specs=[VMEM] * SIDE,
        scratch_shapes=[pltpu.VMEM((2, 2, SIDE, blocks // SIDE, width), f32)],
        compiler_params=pltpu.CompilerParams(vmem_limit_bytes=SMALL),
        name="fold",
    )(*parts)


def finish_kernel(tallies, all_tallies, own, first, second, third, coefficients, energy, mine):
    blocks = coefficients.shape[0]
    total = own[...] + sum(part[...].astype(f32) for part in (first, second, third))
    for c in range(2):
        part = total[:, c * blocks : (c + 1) * blocks]
        coefficients[:, c] = jnp.swapaxes(part, 0, 1)
    start = lax.axis_index("row") * blocks
    total_weight = jnp.sum(all_tallies[...].astype(f32), axis=1, keepdims=True)
    for j in range(blocks):
        weight = tallies[start + j].astype(f32) / total_weight
        real, imag = coefficients[j, 0], coefficients[j, 1]
        power = weight * (real * real + imag * imag)
        mine[...] = power if j == 0 else mine[...] + power
    energy[...] = jnp.broadcast_to(mine[...].astype(bf16)[None], energy.shape)


def output_kernel(parts, coefficients, coefficients_hbm, energy_hbm, energy, sems):
    copy = pltpu.make_async_copy(coefficients, coefficients_hbm, sems.at[0])
    copy.start()
    energy[...] = jnp.sum(parts[...].astype(f32), axis=0)
    last = pltpu.make_async_copy(energy, energy_hbm, sems.at[1])
    last.start()
    copy.wait()
    last.wait()


def shards(snapshots, usable_frame_tallies, retained_frequency_slots, modes):
    row_width = snapshots.shape[1]
    rows = lax.axis_size("row")
    groups = lax.axis_size("block")
    spectra = transform(usable_frame_tallies, retained_frequency_slots, snapshots)

    def along_y(value, distance):
        pairs = [(b, (b + 2 * distance) % groups) for b in range(groups)]
        return lax.ppermute(value, "block", pairs)

    moved = {0: spectra[0]}
    for i in FARTHEST_FIRST:
        moved[i] = along_y(spectra[i], i)

    def along(value, stage, move):
        pairs = []
        for block in range(groups):
            for x in range(SIDE):
                for z in range(SIDE):
                    if (block % 2 == 1) == (stage == 0):
                        target = move(x) * SIDE + z
                    else:
                        target = x * SIDE + move(z)
                    pairs.append((block * rows + x * SIDE + z, block * rows + target))
        return lax.ppermute(value, ("block", "row"), pairs)

    def flipped(value, bits):
        return along(value, 0, lambda place: place ^ bits)

    def onward(value, distance):
        return along(value, 1, lambda place: (place + distance) % SIDE)

    mode_rows = modes.reshape(modes.shape[0], 2 * row_width, modes.shape[3])
    pieces = project([moved[i] for i in range(SIDE)], mode_rows)
    own_a, held_a, direct_a, far_a, own_b, held_b, direct_b, far_b = pieces
    far_a, far_b = flipped(far_a, 1), flipped(far_b, 3)
    direct_a, direct_b = flipped(direct_a, 1), flipped(direct_b, 3)
    relayed_a = flipped(relay(held_a, far_a), 3)
    relayed_b = flipped(relay(held_b, far_b), 1)
    pieces = fold([own_a, direct_a, relayed_a, own_b, direct_b, relayed_b])
    came = {i: onward(pieces[i], i) for i in (1, 3, 2)}
    last = [pieces[0]] + [came[i] for i in range(1, SIDE)]
    freqs, double, width = last[0].shape
    placed = (double // 2, 2, freqs, width)
    coefficients, energy_parts = pl.pallas_call(
        finish_kernel,
        out_shape=[
            jax.ShapeDtypeStruct(placed, f32),
            jax.ShapeDtypeStruct((rows, freqs, width), bf16),
        ],
        in_specs=[SMEM] + [VMEM] * (1 + SIDE),
        out_specs=[VMEM, VMEM],
        scratch_shapes=[pltpu.VMEM((freqs, width), f32)],
        compiler_params=pltpu.CompilerParams(vmem_limit_bytes=SMALL),
        name="finish",
    )(usable_frame_tallies, usable_frame_tallies.reshape(1, -1), *last)
    swapped = lax.all_to_all(energy_parts, "row", 0, 0, tiled=True)
    coefficients, energy = pl.pallas_call(
        output_kernel,
        out_shape=[
            jax.ShapeDtypeStruct(placed, f32),
            jax.ShapeDtypeStruct((freqs, width), f32),
        ],
        in_specs=[VMEM, VMEM],
        out_specs=[pl.BlockSpec(memory_space=pltpu.HBM)] * 2,
        scratch_shapes=[pltpu.VMEM((freqs, width), f32), pltpu.SemaphoreType.DMA((2,))],
        compiler_params=pltpu.CompilerParams(vmem_limit_bytes=SMALL),
        name="output",
    )(swapped, coefficients)
    return (coefficients, energy)


def solution(mesh):
    placed = (P("block", "row"), P(), P(), P("block", None, "row", None))
    return jax.shard_map(
        shards,
        mesh=mesh,
        in_specs=placed,
        out_specs=(P("row", None, "block", None), P("block", None)),
        check_vma=False,
    )
```

```python
import jax
import jax.numpy as jnp
from jax import lax
from jax.experimental import pallas as pl
from jax.experimental.pallas import tpu as pltpu
from jax.sharding import PartitionSpec as P

FRAMES_PER_SEG = 256
FARTHEST_FIRST = (2, 1, 3)
PARTS = 1
SIDE = 4
VMEM = pl.BlockSpec(memory_space=pltpu.VMEM)
SMEM = pl.BlockSpec(memory_space=pltpu.SMEM)
SMALL = 8 << 20
bf16, f32 = jnp.bfloat16, jnp.float32


def windows(tallies, start, blocks):
    spots = lax.broadcasted_iota(jnp.int32, (blocks, FRAMES_PER_SEG), 0)
    lengths = jnp.zeros((blocks, FRAMES_PER_SEG), jnp.int32)
    for j in range(blocks):
        lengths = jnp.where(spots == j, tallies[start + j], lengths)
    times = lax.broadcasted_iota(jnp.int32, (blocks, FRAMES_PER_SEG), 1)
    angle = jnp.pi * (times.astype(f32) + 0.5) / lengths.astype(f32)
    window = jnp.where(times < lengths, jnp.sin(angle) ** 2, 0.0)
    return window * (1.0 / jnp.sqrt(jnp.sum(window * window, axis=1, keepdims=True)))


def transform_blocks(blocks, rows, table, snapshots, acc):
    for j in range(blocks):
        frames = snapshots[j * FRAMES_PER_SEG : (j + 1) * FRAMES_PER_SEG, :]
        acc[pl.ds(j, rows, stride=blocks), :] = jnp.dot(
            table(j), frames, preferred_element_type=f32
        )


def own_kernel(
    tallies_hbm, slots_hbm, snapshots_hbm, spectra, other_tables,
    acc, tallies, slots, snapshots, sems,
):
    copies = [
        pltpu.make_async_copy(tallies_hbm, tallies, sems.at[0]),
        pltpu.make_async_copy(slots_hbm, slots, sems.at[1]),
    ]
    share = snapshots.shape[0] // PARTS
    for part in range(PARTS):
        rows = pl.ds(part * share, share)
        copies.append(
            pltpu.make_async_copy(
                snapshots_hbm.at[rows, :], snapshots.at[rows, :], sems.at[2 + part]
            )
        )
    for copy in copies:
        copy.start()
    copies[0].wait()
    copies[1].wait()
    block = lax.axis_index("block")
    core = block % 2
    blocks = other_tables.shape[0]
    window = windows(tallies, block * blocks, blocks)
    other_window = windows(tallies, (block + 1 - 2 * core) * blocks, blocks)
    times = lax.broadcasted_iota(jnp.int32, (1, FRAMES_PER_SEG), 1)
    turns = lax.dot_general(
        slots[...].astype(f32).astype(bf16),
        times.astype(f32).astype(bf16),
        (((0,), (0,)), ((), ())),
        preferred_element_type=f32,
    )
    turns = turns.reshape(SIDE, 2, -1, FRAMES_PER_SEG)
    turns = jnp.where(core == 0, turns[:, 0], turns[:, 1]).reshape(-1, FRAMES_PER_SEG)
    turns = (turns.astype(jnp.int32) % FRAMES_PER_SEG).astype(f32)
    phase = turns * (2.0 * jnp.pi / FRAMES_PER_SEG)
    waves = jnp.concatenate([jnp.cos(phase), -jnp.sin(phase)], axis=0)

    def table(j):
        return (window[j : j + 1] * waves).astype(bf16)

    for copy in copies[2:]:
        copy.wait()
    transform_blocks(blocks, waves.shape[0], table, snapshots, acc)
    spectra[...] = acc[...].astype(bf16).reshape(spectra.shape)
    for j in range(blocks):
        other_tables[j] = (other_window[j : j + 1] * waves).astype(bf16)


def other_kernel(own, tables, snapshots, *refs):
    outs, acc = refs[:-1], refs[-1]
    block = lax.axis_index("block")
    y, core = block // 2, block % 2
    transform_blocks(*tables.shape[:2], lambda j: tables[j], snapshots, acc)
    _, _, freqs, blocks, points = own.shape
    size = freqs * blocks
    for i in range(SIDE):
        target = (y + i) % SIDE
        for c in range(2):
            rows = pl.ds(pl.multiple_of((c * SIDE + target) * size, size), size)
            outs[i][:, c, core] = own[c, target]
            outs[i][:, c, 1 - core] = acc[rows, :].astype(bf16).reshape(freqs, blocks, points)


def transform(tallies, slots, snapshots):
    blocks, points = snapshots.shape[0] // FRAMES_PER_SEG, snapshots.shape[1]
    freqs = slots.shape[0] // (2 * SIDE)
    rows = 2 * SIDE * freqs
    swap = [(b, b ^ 1) for b in range(lax.axis_size("block"))]
    others = lax.ppermute(snapshots, "block", swap)
    own, tables = pl.pallas_call(
        own_kernel,
        out_shape=[
            jax.ShapeDtypeStruct((2, SIDE, freqs, blocks, points), bf16),
            jax.ShapeDtypeStruct((blocks, rows, FRAMES_PER_SEG), bf16),
        ],
        in_specs=[pl.BlockSpec(memory_space=pltpu.HBM)] * 3,
        out_specs=[VMEM] * 2,
        scratch_shapes=[
            pltpu.VMEM((rows * blocks, points), f32),
            pltpu.SMEM(tallies.shape, jnp.int32),
            pltpu.VMEM((1, slots.shape[0]), jnp.int32),
            pltpu.VMEM(snapshots.shape, bf16),
            pltpu.SemaphoreType.DMA((2 + PARTS,)),
        ],
        compiler_params=pltpu.CompilerParams(vmem_limit_bytes=SMALL),
        name="transform_own",
    )(
        *[
            pltpu.with_memory_space_constraint(v, pltpu.HBM)
            for v in (tallies, slots.reshape(1, -1), snapshots)
        ]
    )
    return pl.pallas_call(
        other_kernel,
        out_shape=[jax.ShapeDtypeStruct((freqs, 2, 2, blocks, points), bf16)] * SIDE,
        in_specs=[VMEM] * 3,
        out_specs=[VMEM] * SIDE,
        scratch_shapes=[pltpu.VMEM((rows * blocks, points), f32)],
        compiler_params=pltpu.CompilerParams(vmem_limit_bytes=SMALL),
        name="transform_other",
    )(own, tables, others)


def places():
    row = lax.axis_index("row")
    x, z = row // SIDE, row % SIDE
    x_first = lax.axis_index("block") % 2 == 1
    return x_first, jnp.where(x_first, x, z), jnp.where(x_first, z, x)


def project_kernel(*refs):
    spectra, modes, outs, acc = refs[:SIDE], refs[SIDE], refs[SIDE + 1 : -1], refs[-1]
    x_first, place, _ = places()
    y = lax.axis_index("block") // 2
    freqs, points, width = spectra[0].shape[0], spectra[0].shape[4], modes.shape[2]
    for k in range(freqs):
        real, imag = (
            jnp.concatenate([part[k, c].reshape(-1, points) for part in spectra], axis=0)
            for c in range(2)
        )
        left = jnp.concatenate(
            [
                jnp.concatenate([real, imag], axis=1),
                jnp.concatenate([imag, -real], axis=1),
            ],
            axis=0,
        )
        slot = k % 2
        acc[slot] = jnp.dot(left, modes[k], preferred_element_type=f32).reshape(acc.shape[1:])
        half = k // (freqs // 2)
        for i, flip in enumerate((0, 3 - 2 * half, 1 + 2 * half, 2)):
            target = place ^ flip
            piece = []
            for j in range(SIDE):
                x = jnp.where(x_first, target, j)
                z = jnp.where(x_first, j, target)
                piece.append(acc[slot, :, (y + SIDE - x) % SIDE * SIDE + z])
            piece = jnp.stack(piece, axis=1)
            out = outs[half * SIDE + i]
            out[k % (freqs // 2)] = piece.reshape(2, -1, width).astype(out.dtype)


def project(spectra, modes):
    freqs, width = modes.shape[0], modes.shape[2]
    blocks = SIDE * spectra[0].shape[2] * spectra[0].shape[3]
    piece = (freqs // 2, 2, blocks // SIDE, width)
    return pl.pallas_call(
        project_kernel,
        out_shape=[jax.ShapeDtypeStruct(piece, t) for t in (f32, f32, bf16, bf16) * 2],
        in_specs=[VMEM] * (SIDE + 1),
        out_specs=[VMEM] * (2 * SIDE),
        scratch_shapes=[pltpu.VMEM((2, 2, SIDE * SIDE, blocks // (SIDE * SIDE), width), f32)],
        compiler_params=pltpu.CompilerParams(vmem_limit_bytes=SMALL),
        name="project",
    )(*spectra, modes)


def relay_kernel(held, came, out):
    out[...] = (held[...] + came[...].astype(f32)).astype(bf16)


def relay(held, came):
    return pl.pallas_call(
        relay_kernel,
        out_shape=jax.ShapeDtypeStruct(came.shape, bf16),
        in_specs=[VMEM] * 2,
        out_specs=VMEM,
        compiler_params=pltpu.CompilerParams(vmem_limit_bytes=SMALL),
        name="relay",
    )(held, came)


def fold_kernel(*refs):
    parts, outs, acc = refs[:6], refs[6:-1], refs[-1]
    _, _, place = places()
    half, width = parts[0].shape[0], parts[0].shape[3]
    for k in range(2 * half):
        own, direct, relayed = parts[3 * (k // half) : 3 * (k // half) + 3]
        total = own[k % half] + direct[k % half].astype(f32) + relayed[k % half].astype(f32)
        acc[k % 2] = total.reshape(acc.shape[1:])
        for i in range(SIDE):
            piece = acc[k % 2, :, (place + i) % SIDE].reshape(-1, width)
            outs[i][k] = piece.astype(outs[i].dtype)


def fold(parts):
    half, _, blocks, width = parts[0].shape
    piece = (2 * half, 2 * blocks // SIDE, width)
    return pl.pallas_call(
        fold_kernel,
        out_shape=[jax.ShapeDtypeStruct(piece, f32 if i == 0 else bf16) for i in range(SIDE)],
        in_specs=[VMEM] * 6,
        out_specs=[VMEM] * SIDE,
        scratch_shapes=[pltpu.VMEM((2, 2, SIDE, blocks // SIDE, width), f32)],
        compiler_params=pltpu.CompilerParams(vmem_limit_bytes=SMALL),
        name="fold",
    )(*parts)


def finish_kernel(tallies, all_tallies, own, first, second, third, coefficients, energy, mine):
    blocks = coefficients.shape[0]
    total = own[...] + sum(part[...].astype(f32) for part in (first, second, third))
    for c in range(2):
        part = total[:, c * blocks : (c + 1) * blocks]
        coefficients[:, c] = jnp.swapaxes(part, 0, 1)
    start = lax.axis_index("row") * blocks
    total_weight = jnp.sum(all_tallies[...].astype(f32), axis=1, keepdims=True)
    for j in range(blocks):
        weight = tallies[start + j].astype(f32) / total_weight
        real, imag = coefficients[j, 0], coefficients[j, 1]
        power = weight * (real * real + imag * imag)
        mine[...] = power if j == 0 else mine[...] + power
    energy[...] = jnp.broadcast_to(mine[...].astype(bf16)[None], energy.shape)


def output_kernel(parts, coefficients, coefficients_hbm, energy_hbm, energy, sems):
    copy = pltpu.make_async_copy(coefficients, coefficients_hbm, sems.at[0])
    copy.start()
    energy[...] = jnp.sum(parts[...].astype(f32), axis=0)
    last = pltpu.make_async_copy(energy, energy_hbm, sems.at[1])
    last.start()
    copy.wait()
    last.wait()


def shards(snapshots, usable_frame_tallies, retained_frequency_slots, modes):
    row_width = snapshots.shape[1]
    rows = lax.axis_size("row")
    groups = lax.axis_size("block")
    spectra = transform(usable_frame_tallies, retained_frequency_slots, snapshots)

    def along_y(value, distance):
        pairs = [(b, (b + 2 * distance) % groups) for b in range(groups)]
        return lax.ppermute(value, "block", pairs)

    moved = {0: spectra[0]}
    for i in FARTHEST_FIRST:
        moved[i] = along_y(spectra[i], i)

    def along(value, stage, move):
        pairs = []
        for block in range(groups):
            for x in range(SIDE):
                for z in range(SIDE):
                    if (block % 2 == 1) == (stage == 0):
                        target = move(x) * SIDE + z
                    else:
                        target = x * SIDE + move(z)
                    pairs.append((block * rows + x * SIDE + z, block * rows + target))
        return lax.ppermute(value, ("block", "row"), pairs)

    def flipped(value, bits):
        return along(value, 0, lambda place: place ^ bits)

    def onward(value, distance):
        return along(value, 1, lambda place: (place + distance) % SIDE)

    mode_rows = modes.reshape(modes.shape[0], 2 * row_width, modes.shape[3])
    pieces = project([moved[i] for i in range(SIDE)], mode_rows)
    own_a, held_a, direct_a, far_a, own_b, held_b, direct_b, far_b = pieces
    far_a, far_b = flipped(far_a, 1), flipped(far_b, 3)
    direct_a, direct_b = flipped(direct_a, 1), flipped(direct_b, 3)
    relayed_a = flipped(relay(held_a, far_a), 3)
    relayed_b = flipped(relay(held_b, far_b), 1)
    pieces = fold([own_a, direct_a, relayed_a, own_b, direct_b, relayed_b])
    came = {i: onward(pieces[i], i) for i in (1, 3, 2)}
    last = [pieces[0]] + [came[i] for i in range(1, SIDE)]
    freqs, double, width = last[0].shape
    placed = (double // 2, 2, freqs, width)
    coefficients, energy_parts = pl.pallas_call(
        finish_kernel,
        out_shape=[
            jax.ShapeDtypeStruct(placed, f32),
            jax.ShapeDtypeStruct((rows, freqs, width), bf16),
        ],
        in_specs=[SMEM] + [VMEM] * (1 + SIDE),
        out_specs=[VMEM, VMEM],
        scratch_shapes=[pltpu.VMEM((freqs, width), f32)],
        compiler_params=pltpu.CompilerParams(vmem_limit_bytes=SMALL),
        name="finish",
    )(usable_frame_tallies, usable_frame_tallies.reshape(1, -1), *last)
    swapped = lax.all_to_all(energy_parts, "row", 0, 0, tiled=True)
    coefficients, energy = pl.pallas_call(
        output_kernel,
        out_shape=[
            jax.ShapeDtypeStruct(placed, f32),
            jax.ShapeDtypeStruct((freqs, width), f32),
        ],
        in_specs=[VMEM, VMEM],
        out_specs=[pl.BlockSpec(memory_space=pltpu.HBM)] * 2,
        scratch_shapes=[pltpu.VMEM((freqs, width), f32), pltpu.SemaphoreType.DMA((2,))],
        compiler_params=pltpu.CompilerParams(vmem_limit_bytes=SMALL),
        name="output",
    )(swapped, coefficients)
    return (coefficients, energy)


def solution(mesh):
    placed = (P("block", "row"), P(), P(), P("block", None, "row", None))
    return jax.shard_map(
        shards,
        mesh=mesh,
        in_specs=placed,
        out_specs=(P("row", None, "block", None), P("block", None)),
        check_vma=False,
    )
```
